128 devices in a mesh: dp: 8 (over z, core), mp: 16 (over x, y).
Axes of the slice: x: 4, y: 4, z: 4, core: 2. Of those that a mesh axis runs over, the one named last changes fastest.
Arguments:
- tokens: bfloat16 [8192, 4096], P('dp', 'mp'), parts along dimension 0, may hold values from -6 to 6
- cotangent: bfloat16 [8192, 4096], P('dp', 'mp'), parts along dimension 0, may hold values from -6 to 6
- offsets: int32 [64], P('dp'), parts along dimension 0, may hold values from 0 to 960, as said below
- w_gate: bfloat16 [4096, 14336], P(None, 'mp'), may hold values from -0.09375 to 0.09375
- w_up: bfloat16 [4096, 14336], P(None, 'mp'), may hold values from -0.09375 to 0.09375
- w_down: bfloat16 [14336, 4096], P('mp'), may hold values from -0.046875 to 0.046875
- feature_proj: bfloat16 [4096, 192], replicated, may hold values from -0.09375 to 0.09375
- hidden_proj: bfloat16 [14336, 192], P('mp'), may hold values from -0.046875 to 0.046875
Outputs:
- input_grad: bfloat16 [4096, 4096], P(('dp', 'mp')), parts along dimension 0
- projected_grads: float32 [3, 64, 64, 64], P(None, 'dp'), parts along dimension 1
The draws below stay inside these ranges and needn't reach their ends.
There are 8 independent parts, one for each index of `dp`. The reference program is written for one: setup_inputs(seed, part) draws one part's arguments, and reference() takes and returns one part's arrays. A program takes and returns all parts, laid end to end along the dimension named above; an argument that names none is the same for every part. Nothing has to cross between parts.
Inputs may be any that keep to these rules, and one draw needn't show every extreme that they name: `offsets`: spans lie inside the batch and may intersect; in every draw some span starts at 0 and some at 960.
All inputs are finite; a program needn't handle non-finite values.
Results may differ from the reference program's by a relative error of at most 0.0049.
Values may be sent and summed in bfloat16 or wider, within the bound.
No kernel may reach another device: no remote copies, remote signals or barrier semaphores. Data moves between devices by JAX's collectives and lax.ppermute only.
A program may use at most 128 MiB of HBM per device.

```python
import jax
import jax.numpy as jnp
from jax import lax

D = 4096
FF = 14336
RANK = 64
SPAN_LEN = 64
SPANS = 8
BATCH_TOK = 1024


def draw_offsets(key, part):
    first_key, second_key = jax.random.split(jax.random.fold_in(key, 11))
    starts = jax.random.randint(first_key, (SPANS,), 0, BATCH_TOK - SPAN_LEN + 1)
    order = jax.random.permutation(second_key, SPANS)
    starts = starts.at[order[0]].set(0)
    starts = starts.at[order[1]].set(BATCH_TOK - SPAN_LEN)
    return starts.astype(jnp.int32)


def shard_levels(key, shape, pieces, least, largest):
    level, own = 1.0, jax.random.fold_in(key, 6)
    for axis_at, shards_of in pieces:
        steps = jnp.exp(jax.random.uniform(jax.random.fold_in(own, axis_at), (shards_of,), jnp.float32, least / len(pieces), largest / len(pieces)))
        level = level * jnp.repeat(steps, shape[axis_at] // shards_of).reshape([-1 if axis == axis_at else 1 for axis in range(len(shape))])
    return level


def scatter_about(key, shape, deviation, limit, cuts=(), kind=jnp.bfloat16):
    values = deviation * jax.random.normal(key, shape, jnp.float32)
    if cuts:
        values = values * shard_levels(key, shape, cuts, -0.22, 0.18)
    return jnp.clip(values, -limit, limit).astype(kind)


def setup_inputs(seed: int = 0, part: int = 0) -> dict:
    splits = jax.random.split(jax.random.key(seed), 9)
    own_keys = jax.random.split(jax.random.fold_in(splits[8], part), 9)
    tokens = scatter_about(own_keys[0], (BATCH_TOK, D), 1.0, 6.0, ((1, 16),))
    cotangent = scatter_about(own_keys[1], (BATCH_TOK, D), 1.0, 6.0, ((1, 16),))
    offsets = draw_offsets(jax.random.fold_in(jax.random.fold_in(splits[8], part), 71), part)
    w_gate = scatter_about(splits[3], (D, FF), D ** -0.5, 0.09375, ((1, 16),))
    w_up = scatter_about(splits[4], (D, FF), D ** -0.5, 0.09375, ((1, 16),))
    w_down = scatter_about(splits[5], (FF, D), FF ** -0.5, 0.046875, ((0, 16),))
    feature_proj = scatter_about(splits[6], (D, 3 * RANK), D ** -0.5, 0.09375)
    hidden_proj = scatter_about(splits[7], (FF, 3 * RANK), FF ** -0.5, 0.046875, ((0, 16),))
    return dict(tokens=tokens, cotangent=cotangent, offsets=offsets, w_gate=w_gate, w_up=w_up, w_down=w_down, feature_proj=feature_proj, hidden_proj=hidden_proj)


def reference(tokens, cotangent, offsets, w_gate, w_up, w_down, feature_proj, hidden_proj):
    positions = (offsets[:, None] + jnp.arange(SPAN_LEN, dtype=jnp.int32)[None, :]).reshape(-1).astype(jnp.int32)
    span_x = jnp.take(tokens, positions, axis=0)
    span_g = jnp.take(cotangent, positions, axis=0)
    pre_gate = jnp.dot(span_x, w_gate, preferred_element_type=jnp.float32)
    pre_up = jnp.dot(span_x, w_up, preferred_element_type=jnp.float32)
    sigmoid_gate = jax.nn.sigmoid(pre_gate)
    activated = pre_gate * sigmoid_gate
    hidden = (activated * pre_up).astype(jnp.bfloat16)
    grad_hidden = jnp.dot(span_g, w_down.T, preferred_element_type=jnp.float32)
    grad_gate = (grad_hidden * pre_up * sigmoid_gate * (1.0 + pre_gate * (1.0 - sigmoid_gate))).astype(jnp.bfloat16)
    grad_up = (grad_hidden * activated).astype(jnp.bfloat16)
    input_grad = (jnp.dot(grad_gate, w_gate.T, preferred_element_type=jnp.float32)
                  + jnp.dot(grad_up, w_up.T, preferred_element_type=jnp.float32)).astype(jnp.bfloat16)
    feat_x = jnp.dot(span_x, feature_proj, preferred_element_type=jnp.float32)
    feat_g = jnp.dot(span_g, feature_proj, preferred_element_type=jnp.float32)
    hid_gate = jnp.dot(grad_gate, hidden_proj[:, :RANK], preferred_element_type=jnp.float32)
    hid_up = jnp.dot(grad_up, hidden_proj[:, RANK:2 * RANK], preferred_element_type=jnp.float32)
    hid_down = jnp.dot(hidden, hidden_proj[:, 2 * RANK:], preferred_element_type=jnp.float32)

    def per_span(left, right):
        return jnp.einsum("slr,slq->srq", left.reshape(SPANS, SPAN_LEN, RANK), right.reshape(SPANS, SPAN_LEN, RANK),
                          precision=lax.Precision.HIGHEST)

    grads_gate = per_span(feat_x[:, :RANK], hid_gate)
    grads_up = per_span(feat_x[:, RANK:2 * RANK], hid_up)
    grads_down = per_span(hid_down, feat_g[:, 2 * RANK:])
    return input_grad, jnp.stack([grads_gate, grads_up, grads_down], axis=0)
```

```python
import jax
import jax.numpy as jnp
from jax import lax
from jax.experimental import pallas as pl
from jax.experimental.pallas import tpu as pltpu
from jax.sharding import PartitionSpec as P

RANK = 64
SPAN_LEN = 64
SPANS = 8
ROWS = SPANS * SPAN_LEN
PIECE = 256
FTILE = 128
NF = 7
FSHARD = NF * FTILE
HALF = 2048
PROJ = 256
BF = jnp.bfloat16
F32 = jnp.float32
NT = (((1,), (1,)), ((), ()))
TN = (((0,), (0,)), ((), ()))


def shift(v, dx, dy):
    pairs = [(4 * x + y, 4 * ((x + dx) % 4) + (y + dy) % 4) for x in range(4) for y in range(4)]
    return lax.ppermute(v, "mp", pairs)


def whole(shape):
    return pl.BlockSpec(shape, lambda *_: (0,) * len(shape))


def gather_kernel(off, tok, cot, xo, go):
    col = lax.broadcasted_iota(jnp.int32, (SPAN_LEN, 128), 1)
    row = lax.broadcasted_iota(jnp.int32, (SPAN_LEN, 128), 0)
    for s in range(SPANS):
        o = off[s]
        start = pl.multiple_of(jnp.minimum((o // 16) * 16, 1024 - 128), 16)
        pick = jnp.where(col == row + (o - start), 1.0, 0.0).astype(BF)
        out = slice(s * SPAN_LEN, (s + 1) * SPAN_LEN)
        xo[out, :] = jnp.dot(pick, tok[pl.ds(start, 128), :], preferred_element_type=F32).astype(BF)
        go[out, :] = jnp.dot(pick, cot[pl.ds(start, 128), :], preferred_element_type=F32).astype(BF)


def gather(offsets, tokens, cotangent):
    o = jax.ShapeDtypeStruct((ROWS, PIECE), BF)
    return pl.pallas_call(
        gather_kernel,
        in_specs=[pl.BlockSpec(memory_space=pltpu.SMEM), pl.BlockSpec(memory_space=pltpu.VMEM),
                  pl.BlockSpec(memory_space=pltpu.VMEM)],
        out_shape=(o, o),
        cost_estimate=pl.CostEstimate(flops=10**8, bytes_accessed=2 * 10**6, transcendentals=0),
        name="span_rows",
    )(offsets, tokens, cotangent)


def stage(me, xp, gp, wg, wu, wd, fpt, acc, hpt=None):
    first, last = acc is None, hpt is not None

    def body(me_ref, *refs):
        refs = list(refs)
        take = lambda n: [refs.pop(0) for _ in range(n)]
        xs, gs, wgs, wus, wds, fxs, fgs = (take(4) for _ in range(7))
        if not first:
            acc_in, feat_in = take(2)
        if last:
            hp, gg_o, gu_o, proj_o, hid, feat = take(6)
        else:
            acc_o, feat = take(2)
        n = pl.program_id(0)
        @pl.when(n == 0)
        def _():
            fx = lax.dot_general(jnp.concatenate([r[...] for r in xs], axis=1), jnp.concatenate([r[...] for r in fxs], axis=1), NT, preferred_element_type=F32)
            fg = lax.dot_general(jnp.concatenate([r[...] for r in gs], axis=1), jnp.concatenate([r[...] for r in fgs], axis=1), NT, preferred_element_type=F32)
            if first:
                feat[:, :128] = fx
                feat[:, 128:192] = fg
            else:
                feat[:, :128] = fx + feat_in[:, :128]
                feat[:, 128:192] = fg + feat_in[:, 128:192]
            if last:
                hid[...] = jnp.zeros_like(hid)

        x = jnp.concatenate([r[...] for r in xs], axis=1)
        g = jnp.concatenate([r[...] for r in gs], axis=1)
        rhs = jnp.concatenate(
            [jnp.concatenate([r[...] for r in wgs], axis=0), jnp.concatenate([r[...] for r in wus], axis=0)], axis=1)
        gate_up = jnp.dot(x, rhs, preferred_element_type=F32)
        down = lax.dot_general(g, jnp.concatenate([r[...] for r in wds], axis=1), NT, preferred_element_type=F32)
        if not first:
            gate_up += acc_in[0, :, :256]
            down += acc_in[0, :, 256:]

        if not last:
            acc_o[0, :, :256] = gate_up
            acc_o[0, :, 256:] = down
            return
        gate, up = gate_up[:, :128], gate_up[:, 128:]
        sig = jax.nn.sigmoid(gate)
        act = gate * sig
        hidden = (act * up).astype(BF)
        grad_gate = (down * up * sig * (1.0 + gate * (1.0 - sig))).astype(BF)
        grad_up = (down * act).astype(BF)
        gg_o[...] = grad_gate
        gu_o[...] = grad_up
        for k, v in enumerate((grad_gate, grad_up, hidden)):
            sl = slice(k * RANK, (k + 1) * RANK)
            hid[:, sl] += lax.dot_general(v, hp[sl, :], NT, preferred_element_type=F32)

        @pl.when(n == NF - 1)
        def _():
            for q in range(4):
                halves = []
                for s in (2 * q, 2 * q + 1):
                    r = slice(s * SPAN_LEN, (s + 1) * SPAN_LEN)
                    left = jnp.concatenate([feat[r, :128], hid[r, 128:192]], axis=1)
                    right = jnp.concatenate([hid[r, :128], feat[r, 128:192]], axis=1)
                    halves.append(lax.dot_general(left, right, TN, precision=lax.Precision.HIGHEST,
                                                  preferred_element_type=F32))
                for k in range(3):
                    d = slice(k * RANK, (k + 1) * RANK)
                    proj_o[q, d, :] = jnp.concatenate([halves[0][d, d], halves[1][d, d]], axis=1).astype(BF)

    def block(d):
        dx, dy = d
        return lambda m: 4 * ((m[0] // 4 + dx) % 4) + (m[0] % 4 + dy) % 4

    def piece(part):
        return pl.BlockSpec((ROWS, PIECE), lambda n, m: (part, 0))

    specs, ops = [], []
    for group in (xp, gp):
        for arr, part, _ in group:
            specs.append(piece(part))
            ops.append(arr)
    bx = [block(d) for _, _, d in xp]
    bg = [block(d) for _, _, d in gp]
    for w in (wg, wu):
        for b in bx:
            specs.append(pl.BlockSpec((PIECE, FTILE), lambda n, m, b=b: (b(m), n)))
            ops.append(w)
    for b in bg:
        specs.append(pl.BlockSpec((FTILE, PIECE), lambda n, m, b=b: (n, b(m))))
        ops.append(wd)
    for b in bx:
        specs.append(pl.BlockSpec((128, PIECE), lambda n, m, b=b: (0, b(m))))
        ops.append(fpt)
    for b in bg:
        specs.append(pl.BlockSpec((RANK, PIECE), lambda n, m, b=b: (2, b(m))))
        ops.append(fpt)
    acc_spec = pl.BlockSpec((1, ROWS, 384), lambda n, m: (n, 0, 0))
    feat_spec = whole((ROWS, 192))
    acc_shape = jax.ShapeDtypeStruct((NF, ROWS, 384), F32)
    feat_shape = jax.ShapeDtypeStruct((ROWS, 192), F32)
    if not first:
        specs += [acc_spec, feat_spec]
        ops += list(acc)
    scratch = []
    if last:
        specs.append(pl.BlockSpec((192, FTILE), lambda n, m: (0, n)))
        ops.append(hpt)
        tile = pl.BlockSpec((ROWS, FTILE), lambda n, m: (0, n))
        out_specs = [tile, tile, whole((4, 192, 128))]
        out_shape = [jax.ShapeDtypeStruct((ROWS, FSHARD), BF)] * 2 + [jax.ShapeDtypeStruct((4, 192, 128), BF)]
        scratch = [pltpu.VMEM((ROWS, 192), F32), pltpu.VMEM((ROWS, 192), F32)]
    else:
        out_specs = [acc_spec, feat_spec]
        out_shape = [acc_shape, feat_shape]
    return pl.pallas_call(
        body,
        grid_spec=pltpu.PrefetchScalarGridSpec(num_scalar_prefetch=1, grid=(NF,), in_specs=specs,
                                               out_specs=out_specs, scratch_shapes=scratch),
        out_shape=out_shape,
        cost_estimate=pl.CostEstimate(flops=3 * 2 * ROWS * 1024 * FSHARD, bytes_accessed=20 * 10**6, transcendentals=0),
        name="forward_last" if last else ("forward_first" if first else "forward_mid"),
    )(me, *ops)


ORDER = (0, 1, 3, 2)


def input_grad(me, gg, gu, wg, wu, base, by_x, proj=None):
    width = HALF + (PROJ if proj is not None else 0)

    def body(me_ref, *refs):
        refs = list(refs)
        gg_r, gu_r, wg_r, wu_r = refs[:4]
        outs, rows = refs[-5:-1], refs[-1]
        n = pl.program_id(0)

        @pl.when(n == 0)
        def _():
            x, y = me_ref[0] // 4, me_ref[0] % 4
            for j, d in enumerate(ORDER):
                if by_x:
                    src = [pl.multiple_of(((x + d) % 4) * 128, 128)]
                    size = 128
                else:
                    src = [pl.multiple_of(128 * b + ((y + d) % 4) * 32, 32) for b in range(4)]
                    size = 32
                for b, at in enumerate(src):
                    dst = slice(j * 128 + b * size, j * 128 + (b + 1) * size)
                    rows[dst, :FSHARD] = gg_r[pl.ds(at, size), :]
                    rows[dst, FSHARD:] = gu_r[pl.ds(at, size), :]
                if proj is not None:
                    block = refs[4][(x + d) % 4]
                    outs[j][:, HALF : HALF + 128] = block[:128]
                    outs[j][:64, HALF + 128 :] = block[128:]
                    outs[j][64:, HALF + 128 :] = jnp.zeros((64, 128), BF)

        rhs = jnp.concatenate([wg_r[...], wu_r[...]], axis=1)
        res = lax.dot_general(rows[...], rhs, NT, preferred_element_type=F32).astype(BF)
        for t in range(2):

            @pl.when(n == t)
            def _():
                for j in range(4):
                    outs[j][:, t * 1024 : (t + 1) * 1024] = res[j * 128 : (j + 1) * 128]

    w_spec = pl.BlockSpec((1024, FSHARD), lambda n, m: (base + n, 0))
    specs = [whole((ROWS, FSHARD)), whole((ROWS, FSHARD)), w_spec, w_spec]
    ops = [gg, gu, wg, wu]
    if proj is not None:
        specs.append(whole((4, 192, 128)))
        ops.append(proj)
    return pl.pallas_call(
        body,
        grid_spec=pltpu.PrefetchScalarGridSpec(
            num_scalar_prefetch=1, grid=(2,), in_specs=specs, out_specs=[whole((128, width))] * 4,
            scratch_shapes=[pltpu.VMEM((ROWS, 2 * FSHARD), BF)]),
        out_shape=[jax.ShapeDtypeStruct((128, width), BF)] * 4,
        cost_estimate=pl.CostEstimate(flops=2 * ROWS * 2 * FSHARD * HALF, bytes_accessed=12 * 10**6, transcendentals=0),
        name="input_grad_x" if by_x else "input_grad_y",
    )(me, *ops)


def middle_sum(me, blocks, with_proj):
    width = blocks[0].shape[1]
    out_width = HALF + (6 * 128 if with_proj else 0)

    def body(me_ref, b0, b1, b2, b3, o0, o1, o2, o3, total):
        mine = me_ref[0] % 4 if with_proj else me_ref[0] // 4
        total[...] = (b0[...].astype(F32) + b1[...].astype(F32) + b2[...].astype(F32) + b3[...].astype(F32))
        for j, (d, o) in enumerate(zip(ORDER, (o0, o1, o2, o3))):
            at = pl.multiple_of(((mine + d) % 4) * 32, 32)
            o[:, :HALF] = total[pl.ds(at, 32), :HALF].astype(BF)
            if with_proj:
                for k in range(6):
                    lane = HALF + 128 * (k // 4)
                    o[:, HALF + k * 128 : HALF + (k + 1) * 128] = total[(k % 4) * 32 : (k % 4 + 1) * 32,
                                                                       lane : lane + 128].astype(BF)

    v = pl.BlockSpec(memory_space=pltpu.VMEM)
    return pl.pallas_call(
        body,
        in_specs=[pl.BlockSpec(memory_space=pltpu.SMEM)] + [v] * 4,
        out_specs=[v] * 4,
        out_shape=[jax.ShapeDtypeStruct((32, out_width), BF)] * 4,
        scratch_shapes=[pltpu.VMEM((128, width), F32)],
        cost_estimate=pl.CostEstimate(flops=10**6, bytes_accessed=3 * 10**6, transcendentals=0),
        name="middle_sum_x" if with_proj else "middle_sum_y",
    )(me, *blocks)


def final_sum_x(me, blocks):
    def body(me_ref, b0, b1, b2, b3, o, p, slots):
        y = me_ref[0] % 4
        o[...] = (b0[:, :HALF].astype(F32) + b1[:, :HALF].astype(F32) + b2[:, :HALF].astype(F32)
                  + b3[:, :HALF].astype(F32)).astype(BF)
        for d, b in zip(ORDER, (b0, b1, b2, b3)):
            slots[(y + 4 - d) % 4] = b[:, HALF:].astype(F32)
        total = ((slots[0] + slots[1]) + (slots[2] + slots[3])).astype(BF)
        for k in range(6):
            p[k * 32 : (k + 1) * 32, :] = total[:, k * 128 : (k + 1) * 128]

    v = pl.BlockSpec(memory_space=pltpu.VMEM)
    return pl.pallas_call(
        body,
        in_specs=[pl.BlockSpec(memory_space=pltpu.SMEM)] + [v] * 4,
        out_specs=[v] * 2,
        out_shape=[jax.ShapeDtypeStruct((32, HALF), BF), jax.ShapeDtypeStruct((192, 128), BF)],
        scratch_shapes=[pltpu.VMEM((4, 32, 6 * 128), F32)],
        cost_estimate=pl.CostEstimate(flops=10**6, bytes_accessed=10**6, transcendentals=0),
        name="final_sum_x",
    )(me, *blocks)


def final_sum_y(left, blocks):
    def body(l, b0, b1, b2, b3, o):
        o[:, :HALF] = l[...]
        o[:, HALF:] = (b0[...].astype(F32) + b1[...].astype(F32) + b2[...].astype(F32) + b3[...].astype(F32)).astype(BF)

    v = pl.BlockSpec(memory_space=pltpu.VMEM)
    return pl.pallas_call(
        body, in_specs=[v] * 5, out_specs=v, out_shape=jax.ShapeDtypeStruct((32, 2 * HALF), BF),
        cost_estimate=pl.CostEstimate(flops=10**6, bytes_accessed=10**6, transcendentals=0),
        name="final_sum_y",
    )(left, *blocks)


def assemble(me, blocks):
    def body(me_ref, b0, b1, b2, b3, o):
        x = me_ref[0] // 4
        for d, b in zip(ORDER, (b0, b1, b2, b3)):
            src = (x + 4 - d) % 4
            for k in range(3):
                for h in range(2):
                    o[k, 2 * src + h] = b[k * 64 : (k + 1) * 64, h * 64 : (h + 1) * 64].astype(F32)

    v = pl.BlockSpec(memory_space=pltpu.VMEM)
    return pl.pallas_call(
        body, in_specs=[pl.BlockSpec(memory_space=pltpu.SMEM)] + [v] * 4, out_specs=v,
        out_shape=jax.ShapeDtypeStruct((3, SPANS, RANK, RANK), F32),
        cost_estimate=pl.CostEstimate(flops=10**6, bytes_accessed=10**6, transcendentals=0),
        name="assemble",
    )(me, *blocks)


def per_device(tokens, cotangent, offsets, w_gate, w_up, w_down, feature_proj, hidden_proj):
    me = lax.axis_index("mp").astype(jnp.int32).reshape(1)
    fpt, hpt = feature_proj.T, hidden_proj.T
    xs, gs = gather(offsets, tokens, cotangent)

    sx = lambda v, d: shift(v, 0, d)
    sy = lambda v, d: shift(v, d, 0)

    def first_axis(own, sh):
        return [own, sh(own, 1), sh(own, -1), sh(own, 2)]

    x1 = first_axis(xs, sx)
    g1 = first_axis(gs, sy)
    pos1 = (0, -1, 1, 2)

    def second_axis(p, sh):
        a = jnp.concatenate([p[0], p[1]], axis=0)
        b = jnp.concatenate([p[2], p[3]], axis=0)
        a_lo, a_hi = sh(a, 1), sh(a, -1)
        b_lo, b_hi = sh(b, 1), sh(b, -1)
        a_far, b_far = sh(a_lo, 1), sh(b_hi, -1)
        return a_lo, a_hi, b_lo, b_hi, a_far, b_far

    xa_lo, xa_hi, xb_lo, xb_hi, xa_far, xb_far = second_axis(x1, sy)
    ga_lo, ga_hi, gb_lo, gb_hi, ga_far, gb_far = second_axis(g1, sx)

    def xpair(arr, which, d):
        return [(arr, i, (d, pos1[2 * which + i])) for i in range(2)]

    def gpair(arr, which, d):
        return [(arr, i, (pos1[2 * which + i], d)) for i in range(2)]

    w = (w_gate, w_up, w_down, fpt)
    acc = stage(me, [(x1[i], 0, (0, pos1[i])) for i in range(4)], [(g1[i], 0, (pos1[i], 0)) for i in range(4)], *w, None)
    acc = stage(me, xpair(xa_lo, 0, -1) + xpair(xa_hi, 0, 1), gpair(ga_lo, 0, -1) + gpair(ga_hi, 0, 1), *w, acc)
    acc = stage(me, xpair(xb_lo, 1, -1) + xpair(xb_hi, 1, 1), gpair(gb_lo, 1, -1) + gpair(gb_hi, 1, 1), *w, acc)
    grad_gate, grad_up, proj = stage(me, xpair(xa_far, 0, 2) + xpair(xb_far, 1, 2),
                                     gpair(ga_far, 0, 2) + gpair(gb_far, 1, 2), *w, acc, hpt)

    bx = input_grad(me, grad_gate, grad_up, w_gate, w_up, 0, True, proj)
    rx = [bx[0]] + [sy(bx[j], d) for j, d in ((1, 1), (2, -1), (3, 2))]
    by = input_grad(me, grad_gate, grad_up, w_gate, w_up, 2, False)
    ry = [by[0]] + [sx(by[j], d) for j, d in ((1, 1), (2, -1), (3, 2))]
    mx = middle_sum(me, rx, True)
    qx = [mx[0]] + [sx(mx[j], d) for j, d in ((1, 1), (2, -1), (3, 2))]
    my = middle_sum(me, ry, False)
    qy = [my[0]] + [sy(my[j], d) for j, d in ((1, 1), (2, -1), (3, 2))]
    left, p = final_sum_x(me, qx)
    ps = [p] + [sy(p, d) for d in (1, -1, 2)]
    return final_sum_y(left, qy), assemble(me, ps)


def solution(mesh):
    in_specs = (
        P("dp", "mp"),
        P("dp", "mp"),
        P("dp"),
        P(None, "mp"),
        P(None, "mp"),
        P("mp", None),
        P(),
        P("mp", None),
    )
    out_specs = (P(("dp", "mp"), None), P(None, "dp", None, None))
    return jax.shard_map(
        per_device, mesh=mesh, in_specs=in_specs, out_specs=out_specs, check_vma=False
    )
```

```python
import jax
import jax.numpy as jnp
from jax import lax
from jax.experimental import pallas as pl
from jax.experimental.pallas import tpu as pltpu
from jax.sharding import PartitionSpec as P

RANK = 64
SPAN_LEN = 64
SPANS = 8
ROWS = SPANS * SPAN_LEN
PIECE = 256
FTILE = 128
NF = 7
FSHARD = NF * FTILE
HALF = 2048
PROJ = 256
BF = jnp.bfloat16
F32 = jnp.float32
NT = (((1,), (1,)), ((), ()))
TN = (((0,), (0,)), ((), ()))


def shift(v, dx, dy):
    pairs = [(4 * x + y, 4 * ((x + dx) % 4) + (y + dy) % 4) for x in range(4) for y in range(4)]
    return lax.ppermute(v, "mp", pairs)


VMEM = pl.BlockSpec(memory_space=pltpu.VMEM)
SMEM = pl.BlockSpec(memory_space=pltpu.SMEM)


def vmem(mib):
    return pltpu.CompilerParams(vmem_limit_bytes=mib << 20)


def gather_kernel(off, me, tok, cot, xo, go, me_o):
    me_o[0] = me[0]
    col = lax.broadcasted_iota(jnp.int32, (SPAN_LEN, 128), 1)
    row = lax.broadcasted_iota(jnp.int32, (SPAN_LEN, 128), 0)
    for s in range(SPANS):
        o = off[s]
        start = pl.multiple_of(jnp.minimum((o // 16) * 16, 1024 - 128), 16)
        pick = jnp.where(col == row + (o - start), 1.0, 0.0).astype(BF)
        out = slice(s * SPAN_LEN, (s + 1) * SPAN_LEN)
        xo[out, :] = jnp.dot(pick, tok[pl.ds(start, 128), :], preferred_element_type=F32).astype(BF)
        go[out, :] = jnp.dot(pick, cot[pl.ds(start, 128), :], preferred_element_type=F32).astype(BF)


def gather(offsets, me, tokens, cotangent):
    o = jax.ShapeDtypeStruct((ROWS, PIECE), BF)
    return pl.pallas_call(
        gather_kernel,
        in_specs=[SMEM, SMEM, VMEM, VMEM],
        out_specs=[VMEM, VMEM, SMEM],
        out_shape=(o, o, jax.ShapeDtypeStruct((1,), jnp.int32)),
        compiler_params=vmem(4),
        cost_estimate=pl.CostEstimate(flops=10**8, bytes_accessed=2 * 10**6, transcendentals=0),
        name="span_rows",
    )(offsets, me, tokens, cotangent)


def load_weights(after, *weights):
    n = len(weights)

    def body(me, *refs):
        srcs, dsts, me_o, sems = refs[:n], refs[n : 2 * n], refs[-2], refs[-1]
        me_o[0] = me[0]
        copies = [pltpu.make_async_copy(a, b, sems.at[i]) for i, (a, b) in enumerate(zip(srcs, dsts))]
        for c in copies:
            c.start()
        for c in copies:
            c.wait()

    hbm = pl.BlockSpec(memory_space=pltpu.HBM)
    return pl.pallas_call(
        body,
        in_specs=[SMEM] + [hbm] * n,
        out_specs=[VMEM] * n + [SMEM],
        out_shape=[jax.ShapeDtypeStruct(w.shape, w.dtype) for w in weights] + [jax.ShapeDtypeStruct((1,), jnp.int32)],
        scratch_shapes=[pltpu.SemaphoreType.DMA((n,))],
        compiler_params=vmem(2),
        cost_estimate=pl.CostEstimate(flops=0, bytes_accessed=25 * 10**6, transcendentals=0),
        name="load_weights",
    )(after, *weights)


def pack(after, a, b):
    def body(_, x, y, o):
        o[:ROWS] = x[...]
        o[ROWS:] = y[...]

    return pl.pallas_call(
        body, in_specs=[SMEM, VMEM, VMEM], out_specs=VMEM, out_shape=jax.ShapeDtypeStruct((2 * ROWS, PIECE), BF),
        compiler_params=vmem(4),
        cost_estimate=pl.CostEstimate(flops=0, bytes_accessed=10**6, transcendentals=0), name="pack")(after, a, b)


def stage(me, xp, gp, wg, wu, wd, fpt, acc, hpt=None):
    first, last = acc is None, hpt is not None
    arrays = []
    for arr, _, _ in xp + gp:
        if not any(arr is q for q in arrays):
            arrays.append(arr)
    where = lambda arr: next(i for i, q in enumerate(arrays) if q is arr)

    def body(me_ref, wg_r, wu_r, wd_r, fp_r, *refs):
        refs = list(refs)
        take = lambda n: [refs.pop(0) for _ in range(n)]
        data = take(len(arrays))
        if not first:
            gu_in, dn_in, feat_in = take(3)
        if last:
            hp, gg_o, gu_o, proj_o, hid, feat = take(6)
        else:
            gu_acc, dn_acc, feat = take(3)
        mx, my = me_ref[0] // 4, me_ref[0] % 4

        def load(group):
            vals, at = [], []
            for arr, part, (dx, dy) in group:
                vals.append(data[where(arr)][part * ROWS : (part + 1) * ROWS, :])
                block = 4 * ((mx + dx + 4) % 4) + (my + dy + 4) % 4
                at.append(pl.multiple_of(block * PIECE, PIECE))
            return jnp.concatenate(vals, axis=1), at

        x, xat = load(xp)
        g, gat = load(gp)
        fx = lax.dot_general(x, jnp.concatenate([fp_r[:128, pl.ds(k, PIECE)] for k in xat], axis=1), NT,
                             preferred_element_type=F32)
        fg = lax.dot_general(g, jnp.concatenate([fp_r[128:, pl.ds(k, PIECE)] for k in gat], axis=1), NT,
                             preferred_element_type=F32)
        feat[:, :128] = fx if first else fx + feat_in[:, :128]
        feat[:, 128:192] = fg if first else fg + feat_in[:, 128:192]
        if last:
            hid[...] = jnp.zeros_like(hid)
        for n0 in range(0, NF, 2):
            cols = min(2, NF - n0) * FTILE
            f = slice(n0 * FTILE, n0 * FTILE + cols)
            down2 = lax.dot_general(g, jnp.concatenate([wd_r[f, pl.ds(k, PIECE)] for k in gat], axis=1), NT,
                                    preferred_element_type=F32)
            if not first:
                down2 += dn_in[:, f]
            if not last:
                dn_acc[:, f] = down2
            for n in range(n0, min(n0 + 2, NF)):
                f = slice(n * FTILE, (n + 1) * FTILE)
                rhs = jnp.concatenate(
                    [jnp.concatenate([w[pl.ds(k, PIECE), f] for k in xat], axis=0) for w in (wg_r, wu_r)], axis=1)
                gate_up = jnp.dot(x, rhs, preferred_element_type=F32)
                if not first:
                    gate_up += gu_in[n]
                if not last:
                    gu_acc[n] = gate_up
                    continue
                gate, up = gate_up[:, :FTILE], gate_up[:, FTILE:]
                down = down2[:, (n - n0) * FTILE : (n - n0 + 1) * FTILE]
                sig = jax.nn.sigmoid(gate)
                act = gate * sig
                hidden = (act * up).astype(BF)
                grad_gate = (down * up * sig * (1.0 + gate * (1.0 - sig))).astype(BF)
                grad_up = (down * act).astype(BF)
                gg_o[:, f] = grad_gate
                gu_o[:, f] = grad_up
                for k, v in enumerate((grad_gate, grad_up, hidden)):
                    sl = slice(k * RANK, (k + 1) * RANK)
                    hid[:, sl] += lax.dot_general(v, hp[sl, f], NT, preferred_element_type=F32)
        if last:
            for q in range(4):
                halves = []
                for s in (2 * q, 2 * q + 1):
                    r = slice(s * SPAN_LEN, (s + 1) * SPAN_LEN)
                    left = jnp.concatenate([feat[r, :128], hid[r, 128:192]], axis=1)
                    right = jnp.concatenate([hid[r, :128], feat[r, 128:192]], axis=1)
                    halves.append(lax.dot_general(left, right, TN, precision=lax.Precision.HIGHEST,
                                                  preferred_element_type=F32))
                for k in range(3):
                    d = slice(k * RANK, (k + 1) * RANK)
                    proj_o[q, d, :] = jnp.concatenate([halves[0][d, d], halves[1][d, d]], axis=1).astype(BF)

    ops = [me, wg, wu, wd, fpt] + arrays
    sums = [jax.ShapeDtypeStruct((NF, ROWS, 256), F32), jax.ShapeDtypeStruct((ROWS, FSHARD), F32),
            jax.ShapeDtypeStruct((ROWS, 192), F32)]
    alias = {}
    if not first:
        if not last:
            alias = {len(ops) + i: i for i in range(3)}
        ops += list(acc)
    scratch = []
    if last:
        ops.append(hpt)
        out_shape = [jax.ShapeDtypeStruct((ROWS, FSHARD), BF)] * 2 + [jax.ShapeDtypeStruct((4, 192, 128), BF)]
        scratch = [pltpu.VMEM((ROWS, 192), F32), pltpu.VMEM((ROWS, 192), F32)]
    else:
        out_shape = sums
    return pl.pallas_call(
        body,
        in_specs=[SMEM] + [VMEM] * (len(ops) - 1),
        out_specs=[VMEM] * 3,
        out_shape=out_shape,
        scratch_shapes=scratch,
        input_output_aliases=alias,
        compiler_params=vmem(10),
        cost_estimate=pl.CostEstimate(flops=3 * 2 * ROWS * 1024 * FSHARD, bytes_accessed=10 * 10**6, transcendentals=0),
        name="forward_last" if last else ("forward_first" if first else "forward_mid"),
    )(*ops)


ORDER = (0, 1, 3, 2)


def input_grad(me, gg, gu, wg, wu, base, by_x, proj=None):
    width = HALF + (PROJ if proj is not None else 0)
    tile = 512

    def body(me_ref, gg_r, gu_r, wg_r, wu_r, *refs):
        outs, rows = refs[-5:-1], refs[-1]
        x, y = me_ref[0] // 4, me_ref[0] % 4
        for j, d in enumerate(ORDER):
            if by_x:
                src = [pl.multiple_of(((x + d) % 4) * 128, 128)]
                size = 128
            else:
                src = [pl.multiple_of(128 * b + ((y + d) % 4) * 32, 32) for b in range(4)]
                size = 32
            for b, at in enumerate(src):
                dst = slice(j * 128 + b * size, j * 128 + (b + 1) * size)
                rows[dst, :FSHARD] = gg_r[pl.ds(at, size), :]
                rows[dst, FSHARD:] = gu_r[pl.ds(at, size), :]
            if proj is not None:
                block = refs[0][(x + d) % 4]
                outs[j][:, HALF : HALF + 128] = block[:128]
                outs[j][:64, HALF + 128 :] = block[128:]
                outs[j][64:, HALF + 128 :] = jnp.zeros((64, 128), BF)
        for t in range(HALF // tile):
            w = slice(base * 1024 + t * tile, base * 1024 + (t + 1) * tile)
            rhs = jnp.concatenate([wg_r[w, :], wu_r[w, :]], axis=1)
            res = lax.dot_general(rows[...], rhs, NT, preferred_element_type=F32).astype(BF)
            for j in range(4):
                outs[j][:, t * tile : (t + 1) * tile] = res[j * 128 : (j + 1) * 128]

    ops = [me, gg, gu, wg, wu] + ([proj] if proj is not None else [])
    return pl.pallas_call(
        body,
        in_specs=[SMEM] + [VMEM] * (len(ops) - 1),
        out_specs=[VMEM] * 4,
        scratch_shapes=[pltpu.VMEM((ROWS, 2 * FSHARD), BF)],
        out_shape=[jax.ShapeDtypeStruct((128, width), BF)] * 4,
        compiler_params=vmem(8),
        cost_estimate=pl.CostEstimate(flops=2 * ROWS * 2 * FSHARD * HALF, bytes_accessed=12 * 10**6, transcendentals=0),
        name="input_grad_x" if by_x else "input_grad_y",
    )(*ops)


def middle_sum(me, blocks, with_proj):
    width = blocks[0].shape[1]
    out_width = HALF + (6 * 128 if with_proj else 0)

    def body(me_ref, b0, b1, b2, b3, o0, o1, o2, o3, total):
        mine = me_ref[0] % 4 if with_proj else me_ref[0] // 4
        total[...] = (b0[...].astype(F32) + b1[...].astype(F32) + b2[...].astype(F32) + b3[...].astype(F32))
        for j, (d, o) in enumerate(zip(ORDER, (o0, o1, o2, o3))):
            at = pl.multiple_of(((mine + d) % 4) * 32, 32)
            o[:, :HALF] = total[pl.ds(at, 32), :HALF].astype(BF)
            if with_proj:
                for k in range(6):
                    lane = HALF + 128 * (k // 4)
                    o[:, HALF + k * 128 : HALF + (k + 1) * 128] = total[(k % 4) * 32 : (k % 4 + 1) * 32,
                                                                       lane : lane + 128].astype(BF)

    v = VMEM
    return pl.pallas_call(
        body,
        in_specs=[SMEM] + [v] * 4,
        out_specs=[v] * 4,
        out_shape=[jax.ShapeDtypeStruct((32, out_width), BF)] * 4,
        scratch_shapes=[pltpu.VMEM((128, width), F32)],
        cost_estimate=pl.CostEstimate(flops=10**6, bytes_accessed=3 * 10**6, transcendentals=0),
        compiler_params=vmem(4),
        name="middle_sum_x" if with_proj else "middle_sum_y",
    )(me, *blocks)


def final_sum_x(me, blocks):
    def body(me_ref, b0, b1, b2, b3, o, p, slots):
        y = me_ref[0] % 4
        o[...] = (b0[:, :HALF].astype(F32) + b1[:, :HALF].astype(F32) + b2[:, :HALF].astype(F32)
                  + b3[:, :HALF].astype(F32)).astype(BF)
        for d, b in zip(ORDER, (b0, b1, b2, b3)):
            slots[(y + 4 - d) % 4] = b[:, HALF:].astype(F32)
        total = ((slots[0] + slots[1]) + (slots[2] + slots[3])).astype(BF)
        for k in range(6):
            p[k * 32 : (k + 1) * 32, :] = total[:, k * 128 : (k + 1) * 128]

    v = VMEM
    return pl.pallas_call(
        body,
        in_specs=[SMEM] + [v] * 4,
        out_specs=[v] * 2,
        out_shape=[jax.ShapeDtypeStruct((32, HALF), BF), jax.ShapeDtypeStruct((192, 128), BF)],
        scratch_shapes=[pltpu.VMEM((4, 32, 6 * 128), F32)],
        cost_estimate=pl.CostEstimate(flops=10**6, bytes_accessed=10**6, transcendentals=0),
        compiler_params=vmem(4),
        name="final_sum_x",
    )(me, *blocks)


def final_sum_y(left, blocks):
    def body(l, b0, b1, b2, b3, o):
        o[:, :HALF] = l[...]
        o[:, HALF:] = (b0[...].astype(F32) + b1[...].astype(F32) + b2[...].astype(F32) + b3[...].astype(F32)).astype(BF)

    v = VMEM
    return pl.pallas_call(
        body, in_specs=[v] * 5, out_specs=v, out_shape=jax.ShapeDtypeStruct((32, 2 * HALF), BF),
        cost_estimate=pl.CostEstimate(flops=10**6, bytes_accessed=10**6, transcendentals=0),
        compiler_params=vmem(4),
        name="final_sum_y",
    )(left, *blocks)


def assemble(me, blocks):
    def body(me_ref, b0, b1, b2, b3, o):
        x = me_ref[0] // 4
        for d, b in zip(ORDER, (b0, b1, b2, b3)):
            src = (x + 4 - d) % 4
            for k in range(3):
                for h in range(2):
                    o[k, 2 * src + h] = b[k * 64 : (k + 1) * 64, h * 64 : (h + 1) * 64].astype(F32)

    v = VMEM
    return pl.pallas_call(
        body, in_specs=[SMEM] + [v] * 4, out_specs=v,
        out_shape=jax.ShapeDtypeStruct((3, SPANS, RANK, RANK), F32),
        cost_estimate=pl.CostEstimate(flops=10**6, bytes_accessed=10**6, transcendentals=0),
        compiler_params=vmem(4),
        name="assemble",
    )(me, *blocks)


def per_device(tokens, cotangent, offsets, w_gate, w_up, w_down, feature_proj, hidden_proj):
    me = lax.axis_index("mp").astype(jnp.int32).reshape(1)
    fpt, hpt = feature_proj.T, hidden_proj.T
    xs, gs, me = gather(offsets, me, tokens, cotangent)

    sx = lambda v, d: shift(v, 0, d)
    sy = lambda v, d: shift(v, d, 0)

    w_gate, w_up, w_down, me = load_weights(me, w_gate, w_up, w_down)

    def first_axis(own, sh):
        return [own, sh(own, 1), sh(own, -1), sh(own, 2)]

    x1 = first_axis(xs, sx)
    g1 = first_axis(gs, sy)
    pos1 = (0, -1, 1, 2)

    def second_axis(p, sh):
        a, b = pack(me, p[0], p[1]), pack(me, p[2], p[3])
        a_lo, a_hi = sh(a, 1), sh(a, -1)
        b_lo, b_hi = sh(b, 1), sh(b, -1)
        a_far, b_far = sh(a_lo, 1), sh(b_hi, -1)
        return a_lo, a_hi, b_lo, b_hi, a_far, b_far

    xa_lo, xa_hi, xb_lo, xb_hi, xa_far, xb_far = second_axis(x1, sy)
    ga_lo, ga_hi, gb_lo, gb_hi, ga_far, gb_far = second_axis(g1, sx)

    def xpair(arr, which, d):
        return [(arr, i, (d, pos1[2 * which + i])) for i in range(2)]

    def gpair(arr, which, d):
        return [(arr, i, (pos1[2 * which + i], d)) for i in range(2)]

    w = (w_gate, w_up, w_down, fpt)
    acc = stage(me, [(x1[i], 0, (0, pos1[i])) for i in range(4)], [(g1[i], 0, (pos1[i], 0)) for i in range(4)], *w, None)
    acc = stage(me, xpair(xa_lo, 0, -1) + xpair(xa_hi, 0, 1), gpair(ga_lo, 0, -1) + gpair(ga_hi, 0, 1), *w, acc)
    acc = stage(me, xpair(xb_lo, 1, -1) + xpair(xb_hi, 1, 1), gpair(gb_lo, 1, -1) + gpair(gb_hi, 1, 1), *w, acc)
    grad_gate, grad_up, proj = stage(me, xpair(xa_far, 0, 2) + xpair(xb_far, 1, 2),
                                     gpair(ga_far, 0, 2) + gpair(gb_far, 1, 2), *w, acc, hpt)

    bx = input_grad(me, grad_gate, grad_up, w_gate, w_up, 0, True, proj)
    rx = [bx[0]] + [sy(bx[j], d) for j, d in ((1, 1), (2, -1), (3, 2))]
    by = input_grad(me, grad_gate, grad_up, w_gate, w_up, 2, False)
    ry = [by[0]] + [sx(by[j], d) for j, d in ((1, 1), (2, -1), (3, 2))]
    mx = middle_sum(me, rx, True)
    qx = [mx[0]] + [sx(mx[j], d) for j, d in ((1, 1), (2, -1), (3, 2))]
    my = middle_sum(me, ry, False)
    qy = [my[0]] + [sy(my[j], d) for j, d in ((1, 1), (2, -1), (3, 2))]
    left, p = final_sum_x(me, qx)
    ps = [p] + [sy(p, d) for d in (1, -1, 2)]
    return final_sum_y(left, qy), assemble(me, ps)


def solution(mesh):
    in_specs = (
        P("dp", "mp"),
        P("dp", "mp"),
        P("dp"),
        P(None, "mp"),
        P(None, "mp"),
        P("mp", None),
        P(),
        P("mp", None),
    )
    out_specs = (P(("dp", "mp"), None), P(None, "dp", None, None))
    return jax.shard_map(
        per_device, mesh=mesh, in_specs=in_specs, out_specs=out_specs, check_vma=False
    )
```
